32 devices in a mesh: samp: 8 (over z, x), state: 4 (over y, core).
Axes of the slice: x: 2, y: 2, z: 4, core: 2. Of those that a mesh axis runs over, the one named last changes fastest.
Arguments:
- energies: bfloat16 [4096, 131072], P('state', 'samp'), may hold values from -12 to 12
- offsets: float32 [4096, 1024], P('state', 'samp'), may hold values from -250 to 250
- counts: int32 [4096], P('state'), may hold values from 1 to 31745, as said below
- labels: int32 [131072], P('samp'), may hold values from 0 to 4095
Outputs:
- free_energy: float32 [4096], P('state')
- own_log_probability: float32 [131072], P('samp')
The draws below stay inside these ranges and needn't reach their ends.
Inputs may be any that keep to these rules, and one draw needn't show every extreme that they name: counts[k] is the number of samples n with labels[n] = k; every state has a sample, state 4096 - 1 has exactly one, and state 0 has the most.
All inputs are finite; a program needn't handle non-finite values.
Results may differ from the reference program's by a relative error of at most 0.0003.
Values sent between devices are 32-bit elements; how exact they have to be, the bound alone decides.
A program may use at most 256 MiB of HBM per device.

```python
import jax
import jax.numpy as jnp
from jax import lax

STATES = 4096
BLOCK = 128
ITERS = 3
SAMPLES = 131072


def labels_and_counts(key):
    base = jax.random.fold_in(key, 4711)
    first, second, third = jax.random.split(base, 3)
    extra = SAMPLES - STATES
    reserved = extra // 4
    picks = jnp.minimum(jax.random.randint(first, (extra,), 1, STATES - 1), jax.random.randint(second, (extra,), 1, STATES - 1))
    picks = jnp.where(jnp.arange(extra, dtype=jnp.int32) < reserved, 0, picks).astype(jnp.int32)
    allof = jnp.concatenate([jnp.arange(STATES, dtype=jnp.int32), picks])
    order = jax.random.permutation(third, SAMPLES)
    labels = allof[order].astype(jnp.int32)
    counts = jax.ops.segment_sum(jnp.ones((SAMPLES,), jnp.int32), labels, num_segments=STATES)
    return (labels, counts.astype(jnp.int32))


def draw_labels(key, part):
    return labels_and_counts(key)[0]


def draw_counts(key, part):
    return labels_and_counts(key)[1]


def draw_offsets(key, part):
    first = jax.random.fold_in(jax.random.fold_in(key, 99), 0)
    nblk = SAMPLES // BLOCK
    rough = 2.0 * jnp.clip(jax.random.normal(first, (STATES, nblk), jnp.float32), -6.0, 6.0)
    return rough


def levels(key, shape, cuts, smallest, largest):
    level, own = 1.0, jax.random.fold_in(key, 6)
    for dim, blocks in cuts:
        steps = jnp.exp(jax.random.uniform(jax.random.fold_in(own, dim), (blocks,), jnp.float32, smallest / len(cuts), largest / len(cuts)))
        level = level * jnp.repeat(steps, shape[dim] // blocks).reshape([-1 if axis == dim else 1 for axis in range(len(shape))])
    return level


def noise(rng, dims, scale, reach, pieces=(), kind=jnp.bfloat16):
    level = levels(rng, dims, pieces, -0.22, 0.18) if pieces else 1.0
    entries = jax.random.normal(rng, dims, jnp.float32) * scale * level
    return jnp.minimum(jnp.maximum(entries, -reach), reach).astype(kind)


def setup_inputs(seed: int = 0) -> dict:
    streams_of = jax.random.split(jax.random.key(seed), 5)
    return {
        "energies": noise(streams_of[0], (STATES, SAMPLES), 2.0, 12.0, ((0, 4), (1, 8))),
        "offsets": draw_offsets(jax.random.fold_in(streams_of[4], 71), 0),
        "counts": draw_counts(jax.random.fold_in(streams_of[4], 71), 0),
        "labels": draw_labels(jax.random.fold_in(streams_of[4], 71), 0),
    }


def energy_rows(energies, offsets, start, rows):
    part = lax.dynamic_slice_in_dim(energies, start, rows, 0).astype(jnp.float32)
    shift = lax.dynamic_slice_in_dim(offsets, start, rows, 0)
    nblk = offsets.shape[1]
    return (part.reshape(rows, nblk, BLOCK) + shift[:, :, None]).reshape(rows, nblk * BLOCK)


def denominator(energies, offsets, logc, free):
    rows = min(256, STATES)
    count = STATES // rows

    def step(carry, index):
        best, total = carry
        start = (index * rows).astype(jnp.int32)
        u = energy_rows(energies, offsets, start, rows)
        lead = lax.dynamic_slice_in_dim(logc + free, start, rows, 0)
        terms = lead[:, None] - u
        newbest = jnp.maximum(best, jnp.max(terms, axis=0))
        total = total * jnp.exp(best - newbest) + jnp.sum(jnp.exp(terms - newbest[None, :]), axis=0)
        return (newbest, total), None

    init = (jnp.full((SAMPLES,), -1e30, jnp.float32), jnp.zeros((SAMPLES,), jnp.float32))
    (best, total), _ = lax.scan(step, init, jnp.arange(count, dtype=jnp.int32))
    return best + jnp.log(total)


def update(energies, offsets, denom):
    rows = min(256, STATES)
    count = STATES // rows

    def one(index):
        start = (index * rows).astype(jnp.int32)
        terms = -energy_rows(energies, offsets, start, rows) - denom[None, :]
        best = jnp.max(terms, axis=1)
        return -(best + jnp.log(jnp.sum(jnp.exp(terms - best[:, None]), axis=1)))

    return lax.map(one, jnp.arange(count, dtype=jnp.int32)).reshape(STATES)


def reference(energies, offsets, counts, labels):
    logc = jnp.log(counts.astype(jnp.float32))
    free = jnp.zeros((STATES,), jnp.float32)
    for step in range(ITERS):
        denom = denominator(energies, offsets, logc, free)
        free = update(energies, offsets, denom)
    denom = denominator(energies, offsets, logc, free)
    picked = jnp.take_along_axis(energies, labels[None, :], axis=0)[0].astype(jnp.float32)
    blocks = (jnp.arange(SAMPLES, dtype=jnp.int32) // BLOCK).astype(jnp.int32)
    picked = picked + offsets[labels, blocks]
    own = logc[labels] + free[labels] - picked - denom
    return free - free[0], own
```

```python
import functools

import jax
import jax.numpy as jnp
from jax import lax
from jax.experimental import pallas as pl
from jax.experimental.pallas import tpu as pltpu
from jax.sharding import PartitionSpec as P

ITERS = 3
SUB = 8
LANE = 128
NT = (((1,), (1,)), ((), ()))


def kernel(ns, np_, nc, eng, off, cnt, lab, free_o, own_o, E, offT, pick, dbuf, obuf, fbuf, abuf, lead_s, m_s, s_s,
           load_sem, dss, drs, oss, ors, fss, frs, ass, ars):
    rows = E.shape[1]
    gw = E.shape[2]
    groups = E.shape[0]
    per = groups // nc
    st = lax.axis_index("state")
    sp = lax.axis_index("samp")

    def load(g):
        return pltpu.make_async_copy(eng.at[:, pl.ds(pl.multiple_of(g * gw, gw), gw)], E.at[g], load_sem.at[g])

    @pl.loop(0, groups)
    def _(g):
        load(g).start()

    barrier = pltpu.get_barrier_semaphore()
    for s in range(1, ns):
        pl.semaphore_signal(barrier, inc=1, device_id={"state": lax.rem(st + s, ns)})
    for s in range(1, np_):
        pl.semaphore_signal(barrier, inc=1, device_id={"samp": lax.rem(sp + s, np_)})

    offT[...] = off[...].T.reshape(groups, SUB, rows)
    logc = jnp.log(cnt[...].astype(jnp.float32))
    lead_s[...] = logc
    pl.semaphore_wait(barrier, ns + np_ - 2)

    rowid = lax.broadcasted_iota(jnp.int32, (SUB, LANE), 0)

    def split(x):
        hi = x.astype(jnp.bfloat16)
        lo = (x - hi.astype(jnp.float32)).astype(jnp.bfloat16)
        return jnp.concatenate([hi, lo], axis=0)

    def dcopy(it, c, s):
        part = dbuf.at[it, st, pl.ds(c * per, per)]
        return pltpu.make_async_remote_copy(
            part, part, dss.at[it, c, s - 1], drs.at[it, c, s - 1], device_id={"state": lax.rem(st + s, ns)})

    def ocopy(c, s):
        part = obuf.at[st, pl.ds(c * per, per)]
        return pltpu.make_async_remote_copy(
            part, part, oss.at[c, s - 1], ors.at[c, s - 1], device_id={"state": lax.rem(st + s, ns)})

    def denom_group(it, g, last):
        a = lead_s[...] - offT[g]
        top = jnp.max(a, axis=1, keepdims=True)
        w = split(jnp.exp(a - top))
        out = jnp.dot(w, E[g], preferred_element_type=jnp.float32)
        out = out[:SUB] + out[SUB:]
        tot = out[:, :LANE]
        for i in range(1, SUB):
            tot = jnp.where(rowid == i, out[:, i * LANE:(i + 1) * LANE], tot)
        dbuf[it, st, g] = top + jnp.log(tot)
        if last:
            label = lab[g] - st * rows
            low = label & (LANE - 1)
            high = label >> 7
            sel = jnp.zeros((SUB, LANE), jnp.float32)
            for h in range(rows // LANE):
                got = jnp.take_along_axis(a[:, h * LANE:(h + 1) * LANE], low, axis=1)
                sel = jnp.where(high == h, got, sel)
            obuf[st, g] = sel - pick[g]

    def exp_group(g):
        load(g).wait()
        for i in range(SUB):
            label = jnp.broadcast_to(lab[g, i:i + 1, :] - st * rows, (16, LANE))
            ids = lax.broadcasted_iota(jnp.int32, (16, LANE), 0)

            def body(k, acc):
                for q in range(8):
                    r0 = pl.multiple_of(k * 128 + q * 16, 16)
                    e = E[g, pl.ds(r0, 16), i * LANE:(i + 1) * LANE].astype(jnp.float32)
                    E[g, pl.ds(r0, 16), i * LANE:(i + 1) * LANE] = jnp.exp(-e).astype(jnp.bfloat16)
                    acc = jnp.where(label - r0 == ids, e, acc)
                return acc

            acc = lax.fori_loop(0, rows // 128, body, jnp.zeros((16, LANE), jnp.float32))
            pick[g, i:i + 1, :] = jnp.sum(acc, axis=0, keepdims=True)

    def denominator(it, last):
        @pl.loop(0, nc)
        def _(c):
            @pl.loop(0, per)
            def _(j):
                g = c * per + j
                if it == 0:
                    exp_group(g)
                denom_group(it, g, last)
            for s in range(1, ns):
                dcopy(it, c, s).start()
                if last:
                    ocopy(c, s).start()

    def join(it, g):
        vals = [dbuf[it, q, g] for q in range(ns)]
        top = functools.reduce(jnp.maximum, vals)
        return top + jnp.log(sum(jnp.exp(v - top) for v in vals))

    def fcopy(it, s):
        return pltpu.make_async_remote_copy(
            fbuf.at[it, sp], fbuf.at[it, sp], fss.at[it, s - 1], frs.at[it, s - 1],
            device_id={"samp": lax.rem(sp + s, np_)})

    def update(it):
        m_s[...] = jnp.full(m_s.shape, -1e30, jnp.float32)
        s_s[...] = jnp.zeros(s_s.shape, jnp.float32)

        @pl.loop(0, nc)
        def _(c):
            for s in range(1, ns):
                dcopy(it, c, s).wait()

            @pl.loop(0, per)
            def _(j):
                g = c * per + j
                d = join(it, g)
                low = jnp.min(d, axis=1, keepdims=True)
                r = jnp.exp(low - d)
                spread = jnp.concatenate([jnp.where(rowid == i, r, 0.0) for i in range(SUB)], axis=1)
                out = lax.dot_general(split(spread), E[g], NT, preferred_element_type=jnp.float32)
                x = jnp.log(out[:SUB] + out[SUB:]) - offT[g] - low
                m = m_s[...]
                new = jnp.maximum(m, x)
                s_s[...] = s_s[...] * jnp.exp(m - new) + jnp.exp(x - new)
                m_s[...] = new

        m = m_s[...]
        top = jnp.max(m, axis=0, keepdims=True)
        fbuf[it, sp] = top + jnp.log(jnp.sum(s_s[...] * jnp.exp(m - top), axis=0, keepdims=True))
        for s in range(1, np_):
            fcopy(it, s).start()
        for s in range(1, np_):
            fcopy(it, s).wait()
        vals = [fbuf[it, q] for q in range(np_)]
        top = functools.reduce(jnp.maximum, vals)
        return -(top + jnp.log(sum(jnp.exp(v - top) for v in vals)))

    free = None
    denominator(0, False)
    for it in range(ITERS):
        free = update(it)
        lead_s[...] = logc + free
        if it < ITERS - 1:
            denominator(it + 1, False)

    def acopy(s):
        return pltpu.make_async_remote_copy(
            abuf.at[st], abuf.at[st], ass.at[s - 1], ars.at[s - 1], device_id={"state": lax.rem(st + s, ns)})

    abuf[st] = free[:, :LANE]
    for s in range(1, ns):
        acopy(s).start()
    denominator(ITERS, True)
    for s in range(1, ns):
        acopy(s).wait()
    free_o[...] = free - abuf[0][:, 0:1]

    @pl.loop(0, nc)
    def _(c):
        for s in range(1, ns):
            dcopy(ITERS, c, s).wait()
            ocopy(c, s).wait()

        @pl.loop(0, per)
        def _(j):
            g = c * per + j
            own_o[g] = sum(obuf[q, g] for q in range(ns)) - join(ITERS, g)


def solution(mesh):
    ns, np_ = mesh.shape["state"], mesh.shape["samp"]

    def shards(energies, offsets, counts, labels):
        rows, width = energies.shape
        nblk = offsets.shape[1]
        groups = nblk // SUB
        gw = width // groups
        nc = 4
        dma = pltpu.SemaphoreType.DMA
        vm = pl.BlockSpec(memory_space=pltpu.VMEM)
        free, own = pl.pallas_call(
            functools.partial(kernel, ns, np_, nc),
            out_shape=(
                jax.ShapeDtypeStruct((1, rows), jnp.float32),
                jax.ShapeDtypeStruct((groups, SUB, LANE), jnp.float32),
            ),
            in_specs=[pl.BlockSpec(memory_space=pl.ANY), vm, vm, vm],
            out_specs=(vm, vm),
            scratch_shapes=[
                pltpu.VMEM((groups, rows, gw), jnp.bfloat16),
                pltpu.VMEM((groups, SUB, rows), jnp.float32),
                pltpu.VMEM((groups, SUB, LANE), jnp.float32),
                pltpu.VMEM((ITERS + 1, ns, groups, SUB, LANE), jnp.float32),
                pltpu.VMEM((ns, groups, SUB, LANE), jnp.float32),
                pltpu.VMEM((ITERS, np_, 1, rows), jnp.float32),
                pltpu.VMEM((ns, 1, LANE), jnp.float32),
                pltpu.VMEM((1, rows), jnp.float32),
                pltpu.VMEM((SUB, rows), jnp.float32),
                pltpu.VMEM((SUB, rows), jnp.float32),
                dma((groups,)),
                dma((ITERS + 1, nc, ns - 1)), dma((ITERS + 1, nc, ns - 1)),
                dma((nc, ns - 1)), dma((nc, ns - 1)),
                dma((ITERS, np_ - 1)), dma((ITERS, np_ - 1)),
                dma((ns - 1,)), dma((ns - 1,)),
            ],
            compiler_params=pltpu.CompilerParams(
                collective_id=0, has_side_effects=True, vmem_limit_bytes=60 * 1024 * 1024),
            name="mbar",
        )(energies, offsets, counts.reshape(1, rows), labels.reshape(groups, SUB, LANE))
        return free.reshape(rows), own.reshape(width)

    return jax.shard_map(
        shards,
        mesh=mesh,
        in_specs=(P("state", "samp"), P("state", "samp"), P("state"), P("samp")),
        out_specs=(P("state"), P("samp")),
        check_vma=False,
    )
```

```python
import functools

import jax
import jax.numpy as jnp
from jax import lax
from jax.experimental import pallas as pl
from jax.experimental.pallas import tpu as pltpu
from jax.sharding import PartitionSpec as P

ITERS = 3
SUB = 8
LANE = 128
NLOG2E = -1.4426950408889634
NT = (((1,), (1,)), ((), ()))


def kernel(ns, np_, nc, eng, off, cnt, lab, free_o, own_o, E, offT, pick, dbuf, obuf, fbuf, abuf, lead_s, m_s, s_s,
           load_sem, dss, drs, oss, ors, fss, frs, ass, ars):
    rows = E.shape[1]
    gw = E.shape[2]
    groups = E.shape[0]
    per = groups // nc
    st = lax.axis_index("state")
    sp = lax.axis_index("samp")

    def load(g):
        return pltpu.make_async_copy(eng.at[:, pl.ds(pl.multiple_of(g * gw, gw), gw)], E.at[g], load_sem.at[g])

    @pl.loop(0, groups)
    def _(g):
        load(g).start()

    barrier = pltpu.get_barrier_semaphore()
    for s in range(1, ns):
        pl.semaphore_signal(barrier, inc=1, device_id={"state": lax.rem(st + s, ns)})
    for s in range(1, np_):
        pl.semaphore_signal(barrier, inc=1, device_id={"samp": lax.rem(sp + s, np_)})

    offT[...] = off[...].T.reshape(groups, SUB, rows)
    logc = jnp.log(cnt[...].astype(jnp.float32))
    lead_s[...] = logc
    pl.semaphore_wait(barrier, ns + np_ - 2)

    rowid = lax.broadcasted_iota(jnp.int32, (SUB, LANE), 0)

    def split(x):
        hi = x.astype(jnp.bfloat16)
        lo = (x - hi.astype(jnp.float32)).astype(jnp.bfloat16)
        return jnp.concatenate([hi, lo], axis=0)

    def dcopy(it, c, s):
        part = dbuf.at[it, st, pl.ds(c * per, per)]
        return pltpu.make_async_remote_copy(
            part, part, dss.at[it, c, s - 1], drs.at[it, c, s - 1], device_id={"state": lax.rem(st + s, ns)})

    def ocopy(c, s):
        part = obuf.at[st, pl.ds(c * per, per)]
        return pltpu.make_async_remote_copy(
            part, part, oss.at[c, s - 1], ors.at[c, s - 1], device_id={"state": lax.rem(st + s, ns)})

    def weights(g):
        a = lead_s[...] - offT[g]
        top = jnp.max(a, axis=1, keepdims=True)
        return a, top, split(jnp.exp(a - top))

    def place(tot, c, out):
        out = out[:SUB] + out[SUB:]
        tot = jnp.where(rowid == 2 * c, out[:, :LANE], tot)
        return jnp.where(rowid == 2 * c + 1, out[:, LANE:], tot)

    def denom_group(it, g, last):
        a, top, w = weights(g)
        tot = jnp.zeros((SUB, LANE), jnp.float32)
        for c in range(SUB // 2):
            out = jnp.dot(w, E[g, :, 2 * c * LANE:2 * (c + 1) * LANE], preferred_element_type=jnp.float32)
            tot = place(tot, c, out)
        dbuf[it, st, g] = top + jnp.log(tot)
        if last:
            label = lab[g] - st * rows
            low = label & (LANE - 1)
            high = label >> 7
            sel = jnp.zeros((SUB, LANE), jnp.float32)
            for h in range(rows // LANE):
                got = jnp.take_along_axis(a[:, h * LANE:(h + 1) * LANE], low, axis=1)
                sel = jnp.where(high == h, got, sel)
            obuf[st, g] = sel - pick[g]

    def first_group(g):
        load(g).wait()
        _, top, w = weights(g)
        tot = jnp.zeros((SUB, LANE), jnp.float32)
        ids = lax.broadcasted_iota(jnp.int32, (16, LANE), 0)
        for c in range(SUB // 2):
            high, low, acc = [], [], []
            for h in range(2):
                label = jnp.broadcast_to(lab[g, 2 * c + h:2 * c + h + 1, :] - st * rows, (16, LANE))
                high.append((label >> 4).astype(jnp.int16))
                low.append(label & 15)
                acc.append(jnp.zeros((16, LANE), jnp.bfloat16))
            out = jnp.zeros((2 * SUB, 2 * LANE), jnp.float32)
            for k in range(rows // 512):
                tiles = []
                for q in range(k * 32, (k + 1) * 32):
                    pair = []
                    for h in range(2):
                        at = (g, slice(q * 16, (q + 1) * 16), slice((2 * c + h) * LANE, (2 * c + h + 1) * LANE))
                        e = E[at]
                        v = jnp.exp2(e.astype(jnp.float32) * NLOG2E).astype(jnp.bfloat16)
                        E[at] = v
                        pair.append(v)
                        acc[h] = jnp.where(high[h] == jnp.int16(q), e, acc[h])
                    tiles.append(jnp.concatenate(pair, axis=1))
                out += jnp.dot(w[:, k * 512:(k + 1) * 512], jnp.concatenate(tiles, axis=0),
                               preferred_element_type=jnp.float32)
            for h in range(2):
                got = jnp.where(low[h] == ids, acc[h].astype(jnp.float32), 0.0)
                pick[g, 2 * c + h:2 * c + h + 1, :] = jnp.sum(got, axis=0, keepdims=True)
            tot = place(tot, c, out)
        dbuf[0, st, g] = top + jnp.log(tot)

    def denominator(it, last):
        @pl.loop(0, nc)
        def _(c):
            @pl.loop(0, per)
            def _(j):
                g = c * per + j
                if it == 0:
                    first_group(g)
                else:
                    denom_group(it, g, last)
            for s in range(1, ns):
                dcopy(it, c, s).start()
                if last:
                    ocopy(c, s).start()

    def join(it, g):
        vals = [dbuf[it, q, g] for q in range(ns)]
        top = functools.reduce(jnp.maximum, vals)
        return top + jnp.log(sum(jnp.exp(v - top) for v in vals))

    def fcopy(it, s):
        return pltpu.make_async_remote_copy(
            fbuf.at[it, sp], fbuf.at[it, sp], fss.at[it, s - 1], frs.at[it, s - 1],
            device_id={"samp": lax.rem(sp + s, np_)})

    def update(it):
        m_s[...] = jnp.full(m_s.shape, -1e30, jnp.float32)
        s_s[...] = jnp.zeros(s_s.shape, jnp.float32)

        @pl.loop(0, nc)
        def _(c):
            for s in range(1, ns):
                dcopy(it, c, s).wait()

            @pl.loop(0, per)
            def _(j):
                g = c * per + j
                d = join(it, g)
                low = jnp.min(d, axis=1, keepdims=True)
                r = jnp.exp(low - d)
                spread = jnp.concatenate([jnp.where(rowid == i, r, 0.0) for i in range(SUB)], axis=1)
                lhs = split(spread)
                for q in range(rows // 256):
                    sl = slice(q * 256, (q + 1) * 256)
                    out = lax.dot_general(lhs, E[g, sl, :], NT, preferred_element_type=jnp.float32)
                    x = jnp.log(out[:SUB] + out[SUB:]) - offT[g, :, sl] - low
                    m = m_s[:, sl]
                    new = jnp.maximum(m, x)
                    s_s[:, sl] = s_s[:, sl] * jnp.exp(m - new) + jnp.exp(x - new)
                    m_s[:, sl] = new

        m = m_s[...]
        top = jnp.max(m, axis=0, keepdims=True)
        fbuf[it, sp] = top + jnp.log(jnp.sum(s_s[...] * jnp.exp(m - top), axis=0, keepdims=True))
        for s in range(1, np_):
            fcopy(it, s).start()
        for s in range(1, np_):
            fcopy(it, s).wait()
        vals = [fbuf[it, q] for q in range(np_)]
        top = functools.reduce(jnp.maximum, vals)
        return -(top + jnp.log(sum(jnp.exp(v - top) for v in vals)))

    free = None
    denominator(0, False)
    for it in range(ITERS):
        free = update(it)
        lead_s[...] = logc + free
        if it < ITERS - 1:
            denominator(it + 1, False)

    def acopy(s):
        return pltpu.make_async_remote_copy(
            abuf.at[st], abuf.at[st], ass.at[s - 1], ars.at[s - 1], device_id={"state": lax.rem(st + s, ns)})

    abuf[st] = free[:, :LANE]
    for s in range(1, ns):
        acopy(s).start()
    denominator(ITERS, True)
    for s in range(1, ns):
        acopy(s).wait()
    free_o[...] = free - abuf[0][:, 0:1]

    @pl.loop(0, nc)
    def _(c):
        for s in range(1, ns):
            dcopy(ITERS, c, s).wait()
            ocopy(c, s).wait()

        @pl.loop(0, per)
        def _(j):
            g = c * per + j
            own_o[g] = sum(obuf[q, g] for q in range(ns)) - join(ITERS, g)


def solution(mesh):
    ns, np_ = mesh.shape["state"], mesh.shape["samp"]

    def shards(energies, offsets, counts, labels):
        rows, width = energies.shape
        nblk = offsets.shape[1]
        groups = nblk // SUB
        gw = width // groups
        nc = 4
        dma = pltpu.SemaphoreType.DMA
        vm = pl.BlockSpec(memory_space=pltpu.VMEM)
        free, own = pl.pallas_call(
            functools.partial(kernel, ns, np_, nc),
            out_shape=(
                jax.ShapeDtypeStruct((1, rows), jnp.float32),
                jax.ShapeDtypeStruct((groups, SUB, LANE), jnp.float32),
            ),
            in_specs=[pl.BlockSpec(memory_space=pl.ANY), vm, vm, vm],
            out_specs=(vm, vm),
            scratch_shapes=[
                pltpu.VMEM((groups, rows, gw), jnp.bfloat16),
                pltpu.VMEM((groups, SUB, rows), jnp.float32),
                pltpu.VMEM((groups, SUB, LANE), jnp.float32),
                pltpu.VMEM((ITERS + 1, ns, groups, SUB, LANE), jnp.float32),
                pltpu.VMEM((ns, groups, SUB, LANE), jnp.float32),
                pltpu.VMEM((ITERS, np_, 1, rows), jnp.float32),
                pltpu.VMEM((ns, 1, LANE), jnp.float32),
                pltpu.VMEM((1, rows), jnp.float32),
                pltpu.VMEM((SUB, rows), jnp.float32),
                pltpu.VMEM((SUB, rows), jnp.float32),
                dma((groups,)),
                dma((ITERS + 1, nc, ns - 1)), dma((ITERS + 1, nc, ns - 1)),
                dma((nc, ns - 1)), dma((nc, ns - 1)),
                dma((ITERS, np_ - 1)), dma((ITERS, np_ - 1)),
                dma((ns - 1,)), dma((ns - 1,)),
            ],
            compiler_params=pltpu.CompilerParams(
                collective_id=0, has_side_effects=True, vmem_limit_bytes=60 * 1024 * 1024),
            name="mbar",
        )(energies, offsets, counts.reshape(1, rows), labels.reshape(groups, SUB, LANE))
        return free.reshape(rows), own.reshape(width)

    return jax.shard_map(
        shards,
        mesh=mesh,
        in_specs=(P("state", "samp"), P("state", "samp"), P("state"), P("samp")),
        out_specs=(P("state"), P("samp")),
        check_vma=False,
    )
```

```python
import functools

import jax
import jax.numpy as jnp
from jax import lax
from jax.experimental import pallas as pl
from jax.experimental.pallas import tpu as pltpu
from jax.sharding import PartitionSpec as P

ITERS = 3
SUB = 8
LANE = 128
NLOG2E = -1.4426950408889634
NT = (((1,), (1,)), ((), ()))


def kernel(ns, np_, nc, eng, off, cnt, lab, free_o, own_o, E, offT, pick, dbuf, obuf, fbuf, abuf, lead_s, m_s, s_s, T, low_s,
           load_sem, dss, drs, oss, ors, fss, frs, ass, ars):
    rows = E.shape[1]
    nm, nv = m_s.shape[1], rows - m_s.shape[1]
    gw = E.shape[2]
    groups = E.shape[0]
    per = groups // nc
    st = lax.axis_index("state")
    sp = lax.axis_index("samp")

    def load(g):
        return pltpu.make_async_copy(eng.at[:, pl.ds(pl.multiple_of(g * gw, gw), gw)], E.at[g], load_sem.at[g])

    @pl.loop(0, groups)
    def _(g):
        load(g).start()

    barrier = pltpu.get_barrier_semaphore()
    for s in range(1, ns):
        pl.semaphore_signal(barrier, inc=1, device_id={"state": lax.rem(st + s, ns)})
    for s in range(1, np_):
        pl.semaphore_signal(barrier, inc=1, device_id={"samp": lax.rem(sp + s, np_)})

    offT[...] = off[...].T.reshape(groups, SUB, rows)
    logc = jnp.log(cnt[...].astype(jnp.float32))
    lead_s[...] = logc
    T[...] = jnp.zeros(T.shape, jnp.float32)
    pl.semaphore_wait(barrier, ns + np_ - 2)

    rowid = lax.broadcasted_iota(jnp.int32, (SUB, LANE), 0)

    def split(x):
        hi = x.astype(jnp.bfloat16)
        lo = (x - hi.astype(jnp.float32)).astype(jnp.bfloat16)
        return jnp.concatenate([hi, lo], axis=0)

    def dcopy(it, c, s):
        part = dbuf.at[it, st, pl.ds(c * per, per)]
        return pltpu.make_async_remote_copy(
            part, part, dss.at[it, c, s - 1], drs.at[it, c, s - 1], device_id={"state": lax.rem(st + s, ns)})

    def ocopy(c, s):
        part = obuf.at[st, pl.ds(c * per, per)]
        return pltpu.make_async_remote_copy(
            part, part, oss.at[c, s - 1], ors.at[c, s - 1], device_id={"state": lax.rem(st + s, ns)})

    def weights(g):
        a = lead_s[...] - offT[g]
        top = jnp.max(a, axis=1, keepdims=True)
        return a, top, split(jnp.exp(a - top))

    def place(tot, c, out):
        out = out[:SUB] + out[SUB:]
        tot = jnp.where(rowid == 2 * c, out[:, :LANE], tot)
        return jnp.where(rowid == 2 * c + 1, out[:, LANE:], tot)

    def denom_group(it, g, last):
        a, top, w = weights(g)
        tot = jnp.zeros((SUB, LANE), jnp.float32)
        for c in range(SUB // 2):
            out = jnp.dot(w, E[g, :, 2 * c * LANE:2 * (c + 1) * LANE], preferred_element_type=jnp.float32)
            tot = place(tot, c, out)
        dbuf[it, st, g] = top + jnp.log(tot)
        if last:
            label = lab[g] - st * rows
            low = label & (LANE - 1)
            high = label >> 7
            sel = jnp.zeros((SUB, LANE), jnp.float32)
            for h in range(rows // LANE):
                got = jnp.take_along_axis(a[:, h * LANE:(h + 1) * LANE], low, axis=1)
                sel = jnp.where(high == h, got, sel)
            obuf[st, g] = sel - pick[g]

    def first_group(g):
        load(g).wait()
        _, top, w = weights(g)
        tot = jnp.zeros((SUB, LANE), jnp.float32)
        ids = lax.broadcasted_iota(jnp.int32, (16, LANE), 0)
        for c in range(SUB // 2):
            high, low, acc = [], [], []
            for h in range(2):
                label = jnp.broadcast_to(lab[g, 2 * c + h:2 * c + h + 1, :] - st * rows, (16, LANE))
                high.append((label >> 4).astype(jnp.int16))
                low.append(label & 15)
                acc.append(jnp.zeros((16, LANE), jnp.bfloat16))
            out = jnp.zeros((2 * SUB, 2 * LANE), jnp.float32)
            for k in range(rows // 512):
                tiles = []
                for q in range(k * 32, (k + 1) * 32):
                    pair = []
                    for h in range(2):
                        at = (g, slice(q * 16, (q + 1) * 16), slice((2 * c + h) * LANE, (2 * c + h + 1) * LANE))
                        e = E[at]
                        v = jnp.exp2(e.astype(jnp.float32) * NLOG2E).astype(jnp.bfloat16)
                        E[at] = v
                        pair.append(v)
                        acc[h] = jnp.where(high[h] == jnp.int16(q), e, acc[h])
                    tiles.append(jnp.concatenate(pair, axis=1))
                out += jnp.dot(w[:, k * 512:(k + 1) * 512], jnp.concatenate(tiles, axis=0),
                               preferred_element_type=jnp.float32)
            for h in range(2):
                got = jnp.where(low[h] == ids, acc[h].astype(jnp.float32), 0.0)
                pick[g, 2 * c + h:2 * c + h + 1, :] = jnp.sum(got, axis=0, keepdims=True)
            tot = place(tot, c, out)
        dbuf[0, st, g] = top + jnp.log(tot)

    def denominator(it, last):
        @pl.loop(0, nc)
        def _(c):
            if it == 0:
                @pl.loop(0, per)
                def _(j):
                    first_group(c * per + j)
            else:
                for j in range(per):
                    denom_group(it, c * per + j, last)
            for s in range(1, ns):
                dcopy(it, c, s).start()
                if last:
                    ocopy(c, s).start()

    def join(it, g):
        vals = [dbuf[it, q, g] for q in range(ns)]
        top = functools.reduce(jnp.maximum, vals)
        return top + jnp.log(sum(jnp.exp(v - top) for v in vals))

    def fcopy(it, s):
        return pltpu.make_async_remote_copy(
            fbuf.at[it, sp], fbuf.at[it, sp], fss.at[it, s - 1], frs.at[it, s - 1],
            device_id={"samp": lax.rem(sp + s, np_)})

    def update_group(it, g):
        d = join(it, g)
        low = jnp.min(d, axis=1, keepdims=True)
        r = jnp.exp(low - d)
        low_s[g] = jnp.broadcast_to(low, (SUB, LANE))
        lhs = split(jnp.concatenate([jnp.where(rowid == i, r, 0.0) for i in range(SUB)], axis=1))
        for q in range(0, nm, 256):
            sl = slice(q, min(nm, q + 256))
            out = lax.dot_general(lhs, E[g, sl, :], NT, preferred_element_type=jnp.float32)
            x = jnp.log(out[:SUB] + out[SUB:]) - offT[g, :, sl] - low
            m = m_s[:, sl]
            new = jnp.maximum(m, x)
            s_s[:, sl] = s_s[:, sl] * jnp.exp(m - new) + jnp.exp(x - new)
            m_s[:, sl] = new
        wide = [jnp.broadcast_to(r[i:i + 1, :], (16, LANE)) for i in range(SUB)]
        lane = lax.broadcasted_iota(jnp.int32, (16, LANE), 1)
        for t in range(0, nv, 16):
            acc = T[t:t + 16, :]
            for i in range(SUB):
                v = E[g, nm + t:nm + t + 16, i * LANE:(i + 1) * LANE].astype(jnp.float32) * wide[i]
                acc = jnp.where(lane == g * SUB + i, jnp.sum(v, axis=1, keepdims=True), acc)
            T[t:t + 16, :] = acc

    def update(it):
        m_s[...] = jnp.full(m_s.shape, -1e30, jnp.float32)
        s_s[...] = jnp.zeros(s_s.shape, jnp.float32)

        @pl.loop(0, nc)
        def _(c):
            for s in range(1, ns):
                dcopy(it, c, s).wait()

            for j in range(per):
                update_group(it, c * per + j)

        m = m_s[...]
        top = jnp.max(m, axis=0, keepdims=True)
        fbuf[it, sp, :, 0:nm] = top + jnp.log(jnp.sum(s_s[...] * jnp.exp(m - top), axis=0, keepdims=True))
        if nv:
            x = jnp.log(T[...].T).reshape(groups, SUB, nv) - offT[:, :, nm:] - low_s[:, :, 0:1]
            top = jnp.max(x, axis=(0, 1), keepdims=True)
            fbuf[it, sp, :, nm:] = (top + jnp.log(jnp.sum(jnp.exp(x - top), axis=(0, 1), keepdims=True)))[0]
        for s in range(1, np_):
            fcopy(it, s).start()
        for s in range(1, np_):
            fcopy(it, s).wait()
        vals = [fbuf[it, q] for q in range(np_)]
        top = functools.reduce(jnp.maximum, vals)
        return -(top + jnp.log(sum(jnp.exp(v - top) for v in vals)))

    free = None
    denominator(0, False)
    for it in range(ITERS):
        free = update(it)
        lead_s[...] = logc + free
        if it < ITERS - 1:
            denominator(it + 1, False)

    def acopy(s):
        return pltpu.make_async_remote_copy(
            abuf.at[st], abuf.at[st], ass.at[s - 1], ars.at[s - 1], device_id={"state": lax.rem(st + s, ns)})

    abuf[st] = free[:, :LANE]
    for s in range(1, ns):
        acopy(s).start()
    denominator(ITERS, True)
    for s in range(1, ns):
        acopy(s).wait()
    free_o[...] = free - abuf[0][:, 0:1]

    @pl.loop(0, nc)
    def _(c):
        for s in range(1, ns):
            dcopy(ITERS, c, s).wait()
            ocopy(c, s).wait()

        @pl.loop(0, per)
        def _(j):
            g = c * per + j
            own_o[g] = sum(obuf[q, g] for q in range(ns)) - join(ITERS, g)


def solution(mesh):
    ns, np_ = mesh.shape["state"], mesh.shape["samp"]

    def shards(energies, offsets, counts, labels):
        rows, width = energies.shape
        nblk = offsets.shape[1]
        groups = nblk // SUB
        gw = width // groups
        nc = 4
        nv = rows // 4 if nblk == LANE else 0
        dma = pltpu.SemaphoreType.DMA
        vm = pl.BlockSpec(memory_space=pltpu.VMEM)
        free, own = pl.pallas_call(
            functools.partial(kernel, ns, np_, nc),
            out_shape=(
                jax.ShapeDtypeStruct((1, rows), jnp.float32),
                jax.ShapeDtypeStruct((groups, SUB, LANE), jnp.float32),
            ),
            in_specs=[pl.BlockSpec(memory_space=pl.ANY), vm, vm, vm],
            out_specs=(vm, vm),
            scratch_shapes=[
                pltpu.VMEM((groups, rows, gw), jnp.bfloat16),
                pltpu.VMEM((groups, SUB, rows), jnp.float32),
                pltpu.VMEM((groups, SUB, LANE), jnp.float32),
                pltpu.VMEM((ITERS + 1, ns, groups, SUB, LANE), jnp.float32),
                pltpu.VMEM((ns, groups, SUB, LANE), jnp.float32),
                pltpu.VMEM((ITERS, np_, 1, rows), jnp.float32),
                pltpu.VMEM((ns, 1, LANE), jnp.float32),
                pltpu.VMEM((1, rows), jnp.float32),
                pltpu.VMEM((SUB, rows - nv), jnp.float32),
                pltpu.VMEM((SUB, rows - nv), jnp.float32),
                pltpu.VMEM((max(nv, 16), LANE), jnp.float32),
                pltpu.VMEM((groups, SUB, LANE), jnp.float32),
                dma((groups,)),
                dma((ITERS + 1, nc, ns - 1)), dma((ITERS + 1, nc, ns - 1)),
                dma((nc, ns - 1)), dma((nc, ns - 1)),
                dma((ITERS, np_ - 1)), dma((ITERS, np_ - 1)),
                dma((ns - 1,)), dma((ns - 1,)),
            ],
            compiler_params=pltpu.CompilerParams(
                collective_id=0, has_side_effects=True, vmem_limit_bytes=60 * 1024 * 1024),
            name="mbar",
        )(energies, offsets, counts.reshape(1, rows), labels.reshape(groups, SUB, LANE))
        return free.reshape(rows), own.reshape(width)

    return jax.shard_map(
        shards,
        mesh=mesh,
        in_specs=(P("state", "samp"), P("state", "samp"), P("state"), P("samp")),
        out_specs=(P("state"), P("samp")),
        check_vma=False,
    )
```
